32 devices in a mesh: dp: 8 (over z, y), tensor: 4 (over x, core).
Axes of the slice: x: 2, y: 2, z: 4, core: 2. Of those that a mesh axis runs over, the one named last changes fastest.
Arguments:
- q_nope: bfloat16 [32, 2, 128, 128], P('dp', None, 'tensor'), parts along dimension 0, may hold values from -6 to 6
- q_rope: bfloat16 [32, 2, 128, 64], P('dp', None, 'tensor'), parts along dimension 0, may hold values from -8 to 8
- w_uk: bfloat16 [128, 128, 512], P('tensor'), may hold values from -0.5 to 0.5
- w_uv: bfloat16 [128, 512, 128], P('tensor'), may hold values from -0.25 to 0.25
- cache_latent: bfloat16 [32, 8192, 512], P('dp', 'tensor'), parts along dimension 0, may hold values from -4 to 4
- cache_rope: bfloat16 [32, 64, 8192], P('dp', None, 'tensor'), parts along dimension 0, may hold values from -14 to 14
- scale_pool: float32 [5, 2048], P(None, ('dp', 'tensor')), parts along dimension 1, may hold values from 0.3 to 3
- block_index: int32 [32, 64], P('dp', 'tensor'), parts along dimension 0, may hold values from 0 to 255, as said below
- lengths: int32 [32], P('dp'), parts along dimension 0, may hold values from 2048 to 8192, as said below
Outputs:
- head_outputs: bfloat16 [32, 2, 128, 128], P('dp', None, 'tensor'), parts along dimension 0
The draws below stay inside these ranges and needn't reach their ends.
There are 8 independent parts, one for each index of `dp`. The reference program is written for one: setup_inputs(seed, part) draws one part's arguments, and reference() takes and returns one part's arrays. A program takes and returns all parts, laid end to end along the dimension named above; an argument that names none is the same for every part. Nothing has to cross between parts.
Inputs may be any that keep to these rules, and one draw needn't show every extreme that they name: `block_index`: every column of the scale table is named by exactly one cache block of the group. `lengths`: in a group of two or more requests, one request is shorter than 4096 and the others are at least 4096 long.
All inputs are finite; a program needn't handle non-finite values.
Results may differ from the reference program's by a relative error of at most 0.012.
Values may be sent and summed in bfloat16 or wider, within the bound.
No kernel may reach another device: no remote copies, remote signals or barrier semaphores. Data moves between devices by JAX's collectives and lax.ppermute only.
A program may use at most 128 MiB of HBM per device.

```python
import math
import jax
import jax.numpy as jnp
from jax import lax

REQS = 4
QTOK = 2
HEADS = 128
NOPE = 128
ROPE = 64
LATENT = 512
VDIM = 128
GROUPS = 5
CTX = 8192
NBLK = 64
POOL = 256


def shared(key):
    base_key = jax.random.fold_in(key, 9173)
    key_d = jax.random.fold_in(base_key, 3)
    pool_order = jax.random.permutation(key_d, POOL).astype(jnp.int32).reshape(REQS, NBLK)
    return pool_order


def draw_lengths(key, part):
    own_key = jax.random.fold_in(key, 57)
    key_a, key_b, key_c = jax.random.split(own_key, 3)
    short_ones = jax.random.randint(key_a, (REQS,), CTX // 4, CTX // 2)
    long_ones = jax.random.randint(key_b, (REQS,), CTX // 2, CTX + 1)
    short_pick = jax.random.randint(key_c, (), 0, REQS)
    which = jnp.arange(REQS, dtype=jnp.int32) == short_pick
    return jnp.where(which, short_ones, long_ones).astype(jnp.int32)


def draw_block_index(key, part):
    pool_order = shared(key)
    return pool_order


def draw_scale_pool(key, part):
    own_key = jax.random.fold_in(key, 31)
    logs_drawn = jax.random.uniform(own_key, (GROUPS, POOL), jnp.float32, math.log(0.3), math.log(3.0))
    values = jnp.exp(logs_drawn)
    return values.astype(jnp.float32)


def draw_q_rope(key, part):
    full_shape = (REQS, QTOK, HEADS, ROPE)
    own_key = jax.random.fold_in(key, 11)
    values = jnp.clip(jax.random.normal(own_key, full_shape, jnp.float32), -4.0, 4.0)
    return values.astype(jnp.bfloat16)


def draw_cache_latent(key, part):
    full_shape = (REQS, CTX, LATENT)
    own_key = jax.random.fold_in(key, 21)
    values = jnp.clip(jax.random.normal(own_key, full_shape, jnp.float32), -4.0, 4.0)
    return values.astype(jnp.bfloat16)


def draw_cache_rope(key, part):
    full_shape = (REQS, ROPE, CTX)
    own_key = jax.random.fold_in(key, 41)
    values = jnp.clip(jax.random.normal(own_key, full_shape, jnp.float32), -4.0, 4.0)
    return values.astype(jnp.bfloat16)


def shard_levels(key, extent, pieces, smallest, high):
    loudness = 1.0
    for axis_at, parts in pieces:
        draws = jax.random.uniform(jax.random.fold_in(jax.random.fold_in(key, 6), axis_at), (parts,), jnp.float32, smallest / len(pieces), high / len(pieces))
        loudness = loudness * jnp.repeat(jnp.exp(draws), extent[axis_at] // parts).reshape((-1,) + (1,) * (len(extent) - 1 - axis_at))
    return loudness


def scatter_about(key, extent, deviation, bound, cuts=(), kind=jnp.bfloat16):
    drawn = jax.random.normal(key, extent, jnp.float32) * deviation
    if len(cuts) > 0:
        drawn = shard_levels(key, extent, cuts, -0.22, 0.18) * drawn
    return jnp.clip(drawn, min=-bound, max=bound).astype(kind)


def setup_inputs(seed: int = 0, part: int = 0) -> dict:
    seeds = jax.random.split(jax.random.key(seed), 10)
    own_keys = jax.random.split(jax.random.fold_in(seeds[9], part), 10)
    q_nope = scatter_about(own_keys[0], (REQS, QTOK, HEADS, NOPE), 1.0, 6.0, ((2, 4),))
    q_rope = draw_q_rope(jax.random.fold_in(jax.random.fold_in(seeds[9], part), 71), part)
    w_uk = scatter_about(seeds[2], (HEADS, NOPE, LATENT), NOPE ** -0.5, 0.5, ((0, 4),))
    w_uv = scatter_about(seeds[3], (HEADS, LATENT, VDIM), LATENT ** -0.5, 0.25, ((0, 4),))
    cache_latent = draw_cache_latent(jax.random.fold_in(jax.random.fold_in(seeds[9], part), 71), part)
    cache_rope = draw_cache_rope(jax.random.fold_in(jax.random.fold_in(seeds[9], part), 71), part)
    scale_pool = draw_scale_pool(jax.random.fold_in(jax.random.fold_in(seeds[9], part), 71), part)
    block_index = draw_block_index(jax.random.fold_in(jax.random.fold_in(seeds[9], part), 71), part)
    lengths = draw_lengths(jax.random.fold_in(jax.random.fold_in(seeds[9], part), 71), part)
    return dict(q_nope=q_nope, q_rope=q_rope, w_uk=w_uk, w_uv=w_uv, cache_latent=cache_latent, cache_rope=cache_rope, scale_pool=scale_pool, block_index=block_index, lengths=lengths)


masked_score = -1e30


def one_request(operands):
    query_latent, query_rope, latent_codes, rope_codes, scales, length = operands
    blocks = scales.shape[1]
    groups = scales.shape[0]
    block_width = latent_codes.shape[0] // blocks
    latent_scale = jnp.transpose(scales[:groups - 1])[:, None, :, None]
    latent_full = (latent_codes.astype(jnp.float32).reshape(blocks, block_width, groups - 1, -1) * latent_scale).astype(jnp.bfloat16).reshape(latent_codes.shape)
    rope_scale = scales[groups - 1][None, :, None]
    rope_full = (rope_codes.astype(jnp.float32).reshape(rope_codes.shape[0], blocks, block_width) * rope_scale).astype(jnp.bfloat16).reshape(rope_codes.shape)
    new_tokens = query_latent.shape[0]
    head_count = query_latent.shape[1]
    latent_rows = query_latent.reshape(new_tokens * head_count, -1)
    rope_rows = query_rope.reshape(new_tokens * head_count, -1)
    scores = jnp.dot(latent_rows, latent_full.T, preferred_element_type=jnp.float32) + jnp.dot(rope_rows, rope_full, preferred_element_type=jnp.float32)
    scores = scores * ((NOPE + ROPE) ** -0.5)
    positions = jnp.arange(CTX, dtype=jnp.int32)
    limits = length - QTOK + jnp.arange(QTOK, dtype=jnp.int32)
    allowed = positions[None, :] <= limits[:, None]
    allowed = jnp.repeat(allowed, head_count, axis=0)
    scores = jnp.where(allowed, scores, masked_score)
    peak_score = jnp.max(scores, axis=1, keepdims=True)
    weights = jnp.exp(scores - peak_score)
    totals = jnp.sum(weights, axis=1, keepdims=True)
    mixture = jnp.dot(weights.astype(jnp.bfloat16), latent_full, preferred_element_type=jnp.float32)
    attended = (mixture / totals).astype(jnp.bfloat16)
    return attended.reshape(new_tokens, head_count, -1)


def reference(q_nope, q_rope, w_uk, w_uv, cache_latent, cache_rope, scale_pool, block_index, lengths):
    query_latent = jnp.einsum("rthn,hnc->rthc", q_nope.astype(jnp.float32), w_uk.astype(jnp.float32)).astype(jnp.bfloat16)
    block_scale = jnp.take(scale_pool, block_index, axis=1)
    per_request = jnp.moveaxis(block_scale, 1, 0)
    attended = lax.map(one_request, (query_latent, q_rope, cache_latent, cache_rope, per_request, lengths))
    head_outputs = jnp.einsum("rthc,hcv->rthv", attended.astype(jnp.float32), w_uv.astype(jnp.float32))
    return head_outputs.astype(jnp.bfloat16)
```

```python
import functools
import math

import jax
import jax.numpy as jnp
from jax import lax
from jax.experimental import pallas as pl
from jax.experimental.pallas import tpu as pltpu
from jax.sharding import PartitionSpec as P

f32, bf16 = jnp.float32, jnp.bfloat16
masked_score = -1e30
VMEM = pl.BlockSpec(memory_space=pltpu.VMEM)
SMEM = pl.BlockSpec(memory_space=pltpu.SMEM)
HBM = pl.BlockSpec(memory_space=pl.ANY)


def prepare_kernel(
    index_ref, scale_ref, latent_hbm, rope_hbm, key_ref, turned_ref, latent, rope, latent_sem, rope_sem
):
    requests, span, width = latent.shape
    blocks = index_ref.shape[1]
    shards, groups, per = scale_ref.shape
    block = span // blocks
    lanes = width // (groups - 1)
    me = lax.axis_index("tensor")

    def copies(r):
        return (
            pltpu.make_async_copy(latent_hbm.at[r], latent.at[r], latent_sem.at[r]),
            pltpu.make_async_copy(rope_hbm.at[r], rope.at[r], rope_sem.at[r]),
        )

    for r in range(requests):
        for copy in copies(r):
            copy.start()

    def one(r, carry):
        for copy in copies(r):
            copy.wait()
        for b in range(blocks):
            column = index_ref[r, b]
            owner, place = lax.div(column, per), lax.rem(column, per)
            shard = lax.rem(me - owner + shards, shards)
            at = pl.ds(b * block, block)
            for g in range(groups - 1):
                part = pl.ds(g * lanes, lanes)
                scaled = (latent[r, at, part].astype(f32) * scale_ref[shard, g, place]).astype(bf16)
                key_ref[r, at, part] = scaled
                turned_ref[r, part, at] = scaled.T
            turned_ref[r, pl.ds(width, rope.shape[1]), at] = (
                rope[r, :, at].astype(f32) * scale_ref[shard, groups - 1, place]
            ).astype(bf16)
        return carry

    lax.fori_loop(0, requests, one, 0)


def prepare(index, scales, latent, rope):
    requests, span, width = latent.shape
    depth = rope.shape[1]
    return pl.pallas_call(
        prepare_kernel,
        in_specs=[SMEM, SMEM, HBM, HBM],
        out_specs=[VMEM, VMEM],
        out_shape=[
            jax.ShapeDtypeStruct((requests, span, width), bf16),
            jax.ShapeDtypeStruct((requests, width + depth, span), bf16),
        ],
        scratch_shapes=[
            pltpu.VMEM(latent.shape, bf16),
            pltpu.VMEM(rope.shape, bf16),
            pltpu.SemaphoreType.DMA((requests,)),
            pltpu.SemaphoreType.DMA((requests,)),
        ],
        compiler_params=pltpu.CompilerParams(vmem_limit_bytes=34 << 20),
        cost_estimate=pl.CostEstimate(flops=20_000_000, bytes_accessed=20_000_000, transcendentals=0),
        name="prepare",
    )(index, scales, latent, rope)


def attend_kernel(
    tokens, factor, limit_ref, qa_ref, qb_ref, ra_ref, rb_ref, key_ref, turned_ref,
    oa_ref, ob_ref, la_ref, lb_ref,
):
    requests, rows, width = qa_ref.shape
    span = key_ref.shape[1]
    heads = rows // tokens

    def one(r, carry):
        query = jnp.concatenate(
            [
                jnp.concatenate([qa_ref[r], ra_ref[r]], axis=1),
                jnp.concatenate([qb_ref[r], rb_ref[r]], axis=1),
            ],
            axis=0,
        )
        scores = jnp.dot(query, turned_ref[r], preferred_element_type=f32) * factor
        position = lax.broadcasted_iota(jnp.int32, (1, span), 1)
        bias = [
            jnp.where(position <= limit_ref[r] + t, 0.0, masked_score).astype(f32) for t in range(tokens)
        ]
        scores = jnp.concatenate(
            [scores[k * heads : (k + 1) * heads] + bias[k % tokens] for k in range(2 * tokens)], axis=0
        )
        peak = jnp.max(scores, axis=1, keepdims=True)
        weights = jnp.exp2(scores - peak)
        total = jnp.sum(weights, axis=1, keepdims=True)
        mixture = jnp.dot(weights.astype(bf16), key_ref[r], preferred_element_type=f32)
        mixture = (mixture / total).astype(bf16)
        oa_ref[r] = mixture[:rows]
        ob_ref[r] = mixture[rows:]
        level = jnp.broadcast_to(peak + jnp.log2(total), (2 * rows, 128)).T[:1]
        la_ref[r] = level[:, :rows]
        lb_ref[r] = level[:, rows:]
        return carry

    lax.fori_loop(0, requests, one, 0)


def attend(limit, qa, qb, ra, rb, key, turned, tokens, factor):
    requests, rows, width = qa.shape
    span = key.shape[1]
    mixed = jax.ShapeDtypeStruct((requests, rows, width), bf16)
    level = jax.ShapeDtypeStruct((requests, 1, rows), f32)
    return pl.pallas_call(
        functools.partial(attend_kernel, tokens, factor),
        in_specs=[SMEM] + [VMEM] * 6,
        out_specs=[VMEM] * 4,
        out_shape=[mixed, mixed, level, level],
        compiler_params=pltpu.CompilerParams(vmem_limit_bytes=34 << 20),
        cost_estimate=pl.CostEstimate(
            flops=4 * requests * rows * span * (2 * width + 64),
            bytes_accessed=requests * span * width * 2,
            transcendentals=2 * requests * rows * span,
        ),
        name="attend",
    )(limit, qa, qb, ra, rb, key, turned)


def weigh(parts, levels):
    top = functools.reduce(jnp.maximum, levels)
    shares = [jnp.exp2(level - top) for level in levels]
    total = functools.reduce(jnp.add, shares)
    columns = [jnp.swapaxes(share / total, 1, 2) for share in shares]
    joined = functools.reduce(
        jnp.add, [part.astype(f32) * column for part, column in zip(parts, columns)]
    )
    return joined, top + jnp.log2(total)


def local(tensor, q_nope, q_rope, w_uk, w_uv, cache_latent, cache_rope, scale_pool, block_index, lengths):
    requests, tokens, heads, nope_width = q_nope.shape
    rope_width = q_rope.shape[3]
    width = w_uk.shape[2]
    span = cache_latent.shape[1]
    rows = tokens * heads
    chips = tensor // 2
    factor = (nope_width + rope_width) ** -0.5 * math.log2(math.e)

    def move(x, chip, core):
        pairs = [
            (i, 2 * ((i // 2 + chip) % chips) + ((i % 2) ^ core))
            for i in range(tensor)
        ]
        return lax.ppermute(x, "tensor", pairs)

    def shift(x, by):
        return lax.ppermute(x, "tensor", [(i, (i + by) % tensor) for i in range(tensor)])

    rope_rows = q_rope.reshape(requests, rows, rope_width)
    scales = jnp.stack([scale_pool] + [shift(scale_pool, d) for d in range(1, tensor)])
    ropes = {
        (d, k): rope_rows if d == 0 and k == 0 else move(rope_rows, d, k)
        for d in range(chips)
        for k in range(2)
    }
    own = (
        jnp.einsum("rthn,hnc->rthc", q_nope, w_uk, preferred_element_type=f32)
        .astype(bf16)
        .reshape(requests, rows, width)
    )
    queries = {(0, 0): own, (0, 1): move(own, 0, 1)}
    for d in range(1, chips):
        queries[d, 0] = move(own, d, 0)
        queries[d, 1] = move(queries[d, 0], 0, 1)
    key, turned = prepare(block_index, scales, cache_latent, cache_rope)
    limit = lengths - tokens - lax.axis_index("tensor") * span

    parts, levels = [], []
    for d in range(chips):
        oa, ob, la, lb = attend(
            limit, queries[d, 0], queries[d, 1], ropes[d, 0], ropes[d, 1], key, turned, tokens, factor
        )
        ob, lb = move(ob, 0, 1), move(lb, 0, 1)
        if d == 0:
            parts += [oa, ob]
            levels += [la, lb]
        else:
            joined, level = weigh([oa, ob], [la, lb])
            parts.append(move(joined.astype(bf16), -d, 0))
            levels.append(move(level, -d, 0))
    attended, _ = weigh(parts, levels)
    attended = attended.astype(bf16).reshape(requests, tokens, heads, width)
    projected = jnp.einsum("rthc,hcv->rthv", attended, w_uv, preferred_element_type=f32)
    return projected.astype(bf16)


def solution(mesh):
    placed = (
        P("dp", None, "tensor", None),
        P("dp", None, "tensor", None),
        P("tensor", None, None),
        P("tensor", None, None),
        P("dp", "tensor", None),
        P("dp", None, "tensor"),
        P(None, ("dp", "tensor")),
        P("dp", "tensor"),
        P("dp"),
    )
    return jax.shard_map(
        functools.partial(local, mesh.shape["tensor"]),
        mesh=mesh,
        in_specs=placed,
        out_specs=P("dp", None, "tensor", None),
        check_vma=False,
    )
```

```python
import functools
import math

import jax
import jax.numpy as jnp
from jax import lax
from jax.experimental import pallas as pl
from jax.experimental.pallas import tpu as pltpu
from jax.sharding import PartitionSpec as P

f32, bf16 = jnp.float32, jnp.bfloat16
masked_score = -1e30
VMEM = pl.BlockSpec(memory_space=pltpu.VMEM)
SMEM = pl.BlockSpec(memory_space=pltpu.SMEM)
HBM = pl.BlockSpec(memory_space=pltpu.HBM)


def prepare_kernel(
    index_ref, scale_ref, latent_hbm, rope_hbm, key_ref, turned_ref, latent, rope, latent_sem, rope_sem
):
    requests, span, width = latent.shape
    blocks = index_ref.shape[1]
    shards, groups, per = scale_ref.shape
    block = span // blocks
    lanes = width // (groups - 1)
    me = lax.axis_index("tensor")
    chips = shards // 2

    def copies(r):
        return (
            pltpu.make_async_copy(latent_hbm.at[r], latent.at[r], latent_sem.at[r]),
            pltpu.make_async_copy(rope_hbm.at[r], rope.at[r], rope_sem.at[r]),
        )

    for r in range(requests):
        for copy in copies(r):
            copy.start()

    def one(r, carry):
        for copy in copies(r):
            copy.wait()
        for b in range(blocks):
            column = index_ref[r, b]
            owner, place = lax.div(column, per), lax.rem(column, per)
            turn = lax.rem(me // 2 - owner // 2 + chips, chips)
            other = (me - owner) & 1
            shard = jnp.where(turn == 0, other, turn + 1 + other * (chips - 1))
            at = pl.ds(b * block, block)
            for g in range(groups - 1):
                part = pl.ds(g * lanes, lanes)
                scaled = (latent[r, at, part].astype(f32) * scale_ref[shard, g, place]).astype(bf16)
                key_ref[r, at, part] = scaled
                turned_ref[r, part, at] = scaled.T
            turned_ref[r, pl.ds(width, rope.shape[1]), at] = (
                rope[r, :, at].astype(f32) * scale_ref[shard, groups - 1, place]
            ).astype(bf16)
        return carry

    lax.fori_loop(0, requests, one, 0)


def prepare(index, scales, latent, rope):
    requests, span, width = latent.shape
    depth = rope.shape[1]
    return pl.pallas_call(
        prepare_kernel,
        in_specs=[SMEM, SMEM, HBM, HBM],
        out_specs=[VMEM, VMEM],
        out_shape=[
            jax.ShapeDtypeStruct((requests, span, width), bf16),
            jax.ShapeDtypeStruct((requests, width + depth, span), bf16),
        ],
        scratch_shapes=[
            pltpu.VMEM(latent.shape, bf16),
            pltpu.VMEM(rope.shape, bf16),
            pltpu.SemaphoreType.DMA((requests,)),
            pltpu.SemaphoreType.DMA((requests,)),
        ],
        compiler_params=pltpu.CompilerParams(vmem_limit_bytes=14 << 20),
        cost_estimate=pl.CostEstimate(flops=20_000_000, bytes_accessed=20_000_000, transcendentals=0),
        name="prepare",
    )(
        index,
        scales,
        pltpu.with_memory_space_constraint(latent, pltpu.HBM),
        pltpu.with_memory_space_constraint(rope, pltpu.HBM),
    )


def attend_kernel(
    tokens, factor, limit_ref, qa_ref, qb_ref, ra_ref, rb_ref, key_ref, turned_ref,
    oa_ref, ob_ref, la_ref, lb_ref,
):
    requests, rows, width = qa_ref.shape
    span = key_ref.shape[1]
    heads = rows // tokens

    position = lax.broadcasted_iota(jnp.int32, (1, span), 1)

    def score(r):
        query = jnp.concatenate(
            [
                jnp.concatenate([qa_ref[r], ra_ref[r]], axis=1),
                jnp.concatenate([qb_ref[r], rb_ref[r]], axis=1),
            ],
            axis=0,
        )
        return jnp.dot(query, turned_ref[r], preferred_element_type=f32)

    ahead = score(0)
    for r in range(requests):
        scores = ahead * factor
        if r + 1 < requests:
            ahead = score(r + 1)
        bias = [
            jnp.where(position <= limit_ref[r] + t, 0.0, masked_score).astype(f32) for t in range(tokens)
        ]
        scores = jnp.concatenate(
            [scores[k * heads : (k + 1) * heads] + bias[k % tokens] for k in range(2 * tokens)], axis=0
        )
        peak = jnp.max(scores, axis=1, keepdims=True)
        weights = jnp.exp2(scores - peak)
        total = jnp.sum(weights, axis=1, keepdims=True)
        mixture = jnp.dot(weights.astype(bf16), key_ref[r], preferred_element_type=f32)
        mixture = (mixture * (1.0 / total)).astype(bf16)
        oa_ref[r] = mixture[:rows]
        ob_ref[r] = mixture[rows:]
        level = jnp.broadcast_to(peak + jnp.log2(total), (2 * rows, 128)).T[:1]
        la_ref[r] = level[:, :rows]
        lb_ref[r] = level[:, rows:]


def attend(limit, qa, qb, ra, rb, key, turned, tokens, factor):
    requests, rows, width = qa.shape
    span = key.shape[1]
    mixed = jax.ShapeDtypeStruct((requests, rows, width), bf16)
    level = jax.ShapeDtypeStruct((requests, 1, rows), f32)
    return pl.pallas_call(
        functools.partial(attend_kernel, tokens, factor),
        in_specs=[SMEM] + [VMEM] * 6,
        out_specs=[VMEM] * 4,
        out_shape=[mixed, mixed, level, level],
        compiler_params=pltpu.CompilerParams(vmem_limit_bytes=14 << 20),
        cost_estimate=pl.CostEstimate(
            flops=4 * requests * rows * span * (2 * width + 64),
            bytes_accessed=requests * span * width * 2,
            transcendentals=2 * requests * rows * span,
        ),
        name="attend",
    )(limit, qa, qb, ra, rb, key, turned)


def weigh(parts, levels):
    top = functools.reduce(jnp.maximum, levels)
    shares = [jnp.exp2(level - top) for level in levels]
    total = functools.reduce(jnp.add, shares)
    columns = [jnp.swapaxes(share / total, 1, 2) for share in shares]
    joined = functools.reduce(
        jnp.add, [part.astype(f32) * column for part, column in zip(parts, columns)]
    )
    return joined, top + jnp.log2(total)


def local(tensor, q_nope, q_rope, w_uk, w_uv, cache_latent, cache_rope, scale_pool, block_index, lengths):
    requests, tokens, heads, nope_width = q_nope.shape
    rope_width = q_rope.shape[3]
    width = w_uk.shape[2]
    span = cache_latent.shape[1]
    rows = tokens * heads
    chips = tensor // 2
    factor = (nope_width + rope_width) ** -0.5 * math.log2(math.e)

    def move(x, chip, core):
        pairs = [
            (i, 2 * ((i // 2 + chip) % chips) + ((i % 2) ^ core))
            for i in range(tensor)
        ]
        return lax.ppermute(x, "tensor", pairs)

    def spread(x):
        found = {(0, 0): x, (0, 1): move(x, 0, 1)}
        for d in range(1, chips):
            found[d, 0] = move(x, d, 0)
        for d in range(1, chips):
            found[d, 1] = move(found[d, 0], 0, 1)
        return found

    scales = jnp.stack(list(spread(scale_pool).values()))
    ropes = spread(q_rope.reshape(requests, rows, rope_width))
    own = (
        jnp.einsum("rthn,hnc->rthc", q_nope, w_uk, preferred_element_type=f32)
        .astype(bf16)
        .reshape(requests, rows, width)
    )
    queries = spread(own)
    key, turned = prepare(block_index, scales, cache_latent, cache_rope)
    limit = lengths - tokens - lax.axis_index("tensor") * span

    parts, levels = [], []
    for d in range(chips):
        oa, ob, la, lb = attend(
            limit, queries[d, 0], queries[d, 1], ropes[d, 0], ropes[d, 1], key, turned, tokens, factor
        )
        ob, lb = move(ob, 0, 1), move(lb, 0, 1)
        if d == 0:
            parts += [oa, ob]
            levels += [la, lb]
        else:
            joined, level = weigh([oa, ob], [la, lb])
            parts.append(move(joined.astype(bf16), -d, 0))
            levels.append(move(level, -d, 0))
    attended, _ = weigh(parts, levels)
    attended = attended.astype(bf16).reshape(requests, tokens, heads, width)
    projected = jnp.einsum("rthc,hcv->rthv", attended, w_uv, preferred_element_type=f32)
    return projected.astype(bf16)


def solution(mesh):
    placed = (
        P("dp", None, "tensor", None),
        P("dp", None, "tensor", None),
        P("tensor", None, None),
        P("tensor", None, None),
        P("dp", "tensor", None),
        P("dp", None, "tensor"),
        P(None, ("dp", "tensor")),
        P("dp", "tensor"),
        P("dp"),
    )
    return jax.shard_map(
        functools.partial(local, mesh.shape["tensor"]),
        mesh=mesh,
        in_specs=placed,
        out_specs=P("dp", None, "tensor", None),
        check_vma=False,
    )
```

```python
import functools
import math

import jax
import jax.numpy as jnp
from jax import lax
from jax.experimental import pallas as pl
from jax.experimental.pallas import tpu as pltpu
from jax.sharding import PartitionSpec as P


f32, bf16 = jnp.float32, jnp.bfloat16
masked_score = -1e30
VMEM = pl.BlockSpec(memory_space=pltpu.VMEM)
SMEM = pl.BlockSpec(memory_space=pltpu.SMEM)
HBM = pl.BlockSpec(memory_space=pltpu.HBM)


def prepare_kernel(
    first, pieces, index_ref, scale_ref, latent_hbm, rope_hbm, key_ref, turned_ref, latent, rope, latent_sem, rope_sem
):
    requests, span, width = latent.shape
    blocks = index_ref.shape[1]
    shards, groups, per = scale_ref.shape
    block = span // blocks
    lanes = width // (groups - 1)
    me = lax.axis_index("tensor")
    chips = shards // 2
    step = blocks // pieces

    def latent_copy(r, p):
        at = pl.ds(p * step * block, step * block)
        return pltpu.make_async_copy(
            latent_hbm.at[first + r, at], latent.at[r, at], latent_sem.at[r, p]
        )

    def rope_copy(r):
        return pltpu.make_async_copy(rope_hbm.at[first + r], rope.at[r], rope_sem.at[r])

    for r in range(requests):
        rope_copy(r).start()
        for p in range(pieces):
            latent_copy(r, p).start()

    for r in range(requests):
        rope_copy(r).wait()
        for p in range(pieces):
            latent_copy(r, p).wait()
            for b in range(p * step, (p + 1) * step):
                column = index_ref[first + r, b]
                owner, place = lax.div(column, per), lax.rem(column, per)
                turn = lax.rem(me // 2 - owner // 2 + chips, chips)
                other = (me - owner) & 1
                shard = jnp.where(turn == 0, other, turn + 1 + other * (chips - 1))
                at = pl.ds(b * block, block)
                for g in range(groups - 1):
                    part = pl.ds(g * lanes, lanes)
                    scaled = (latent[r, at, part].astype(f32) * scale_ref[shard, g, place]).astype(bf16)
                    key_ref[r, at, part] = scaled
                    turned_ref[r, part, at] = scaled.T
                turned_ref[r, pl.ds(width, rope.shape[1]), at] = (
                    rope[r, :, at].astype(f32) * scale_ref[shard, groups - 1, place]
                ).astype(bf16)


def prepare(first, requests, index, scales, latent, rope):
    span, width = latent.shape[1:]
    depth = rope.shape[1]
    pieces = 1
    return pl.pallas_call(
        functools.partial(prepare_kernel, first, pieces),
        in_specs=[SMEM, SMEM, HBM, HBM],
        out_specs=[VMEM, VMEM],
        out_shape=[
            jax.ShapeDtypeStruct((requests, span, width), bf16),
            jax.ShapeDtypeStruct((requests, width + depth, span), bf16),
        ],
        scratch_shapes=[
            pltpu.VMEM((requests, span, width), bf16),
            pltpu.VMEM((requests, depth, span), bf16),
            pltpu.SemaphoreType.DMA((requests, pieces)),
            pltpu.SemaphoreType.DMA((requests,)),
        ],
        compiler_params=pltpu.CompilerParams(vmem_limit_bytes=12 << 20),
        cost_estimate=pl.CostEstimate(flops=20_000_000, bytes_accessed=20_000_000, transcendentals=0),
        name="prepare",
    )(
        index,
        scales,
        pltpu.with_memory_space_constraint(latent, pltpu.HBM),
        pltpu.with_memory_space_constraint(rope, pltpu.HBM),
    )


def attend_kernel(
    first, tokens, factor, length_ref, qa_ref, qb_ref, ra_ref, rb_ref, key_ref, turned_ref, after_ref,
    oa_ref, ob_ref, la_ref, lb_ref,
):
    requests, _, rows = la_ref.shape
    span = key_ref.shape[1]
    heads = rows // tokens

    position = lax.broadcasted_iota(jnp.int32, (1, span), 1)

    def score(r):
        query = jnp.concatenate(
            [
                jnp.concatenate([qa_ref[first + r], ra_ref[first + r]], axis=1),
                jnp.concatenate([qb_ref[first + r], rb_ref[first + r]], axis=1),
            ],
            axis=0,
        )
        return jnp.dot(query, turned_ref[first + r], preferred_element_type=f32)

    ahead = score(0)
    for r in range(requests):
        scores = ahead * factor
        if r + 1 < requests:
            ahead = score(r + 1)
        limit = length_ref[first + r] - tokens - lax.axis_index("tensor") * span
        bias = [
            jnp.where(position <= limit + t, 0.0, masked_score).astype(f32) for t in range(tokens)
        ]
        scores = jnp.concatenate(
            [scores[k * heads : (k + 1) * heads] + bias[k % tokens] for k in range(2 * tokens)], axis=0
        )
        peak = jnp.max(scores, axis=1, keepdims=True)
        weights = jnp.exp2(scores - peak)
        total = jnp.sum(weights, axis=1, keepdims=True)
        mixture = jnp.dot(weights.astype(bf16), key_ref[first + r], preferred_element_type=f32)
        mixture = (mixture * (1.0 / total)).astype(bf16)
        oa_ref[r] = mixture[:rows]
        ob_ref[r] = mixture[rows:]
        level = jnp.broadcast_to(peak + jnp.log2(total), (2 * rows, 128)).T[:1]
        la_ref[r] = level[:, :rows]
        lb_ref[r] = level[:, rows:]


def attend(first, requests, lengths, qa, qb, ra, rb, key, turned, after, tokens, factor):
    _, rows, width = qa.shape
    span = key.shape[1]
    mixed = jax.ShapeDtypeStruct((requests, rows, width), bf16)
    level = jax.ShapeDtypeStruct((requests, 1, rows), f32)
    return pl.pallas_call(
        functools.partial(attend_kernel, first, tokens, factor),
        in_specs=[SMEM] + [VMEM] * 6 + [pl.BlockSpec(memory_space=pl.ANY)],
        out_specs=[VMEM] * 4,
        out_shape=[mixed, mixed, level, level],
        compiler_params=pltpu.CompilerParams(vmem_limit_bytes=8 << 20),
        cost_estimate=pl.CostEstimate(
            flops=4 * requests * rows * span * (2 * width + 64),
            bytes_accessed=requests * span * width * 2,
            transcendentals=2 * requests * rows * span,
        ),
        name="attend",
    )(lengths, qa, qb, ra, rb, key, turned, after)


def weigh(parts, levels):
    top = functools.reduce(jnp.maximum, levels)
    shares = [jnp.exp2(level - top) for level in levels]
    total = functools.reduce(jnp.add, shares)
    columns = [jnp.swapaxes(share / total, 1, 2) for share in shares]
    joined = functools.reduce(
        jnp.add, [part.astype(f32) * column for part, column in zip(parts, columns)]
    )
    return joined, top + jnp.log2(total)


def local(tensor, q_nope, q_rope, w_uk, w_uv, cache_latent, cache_rope, scale_pool, block_index, lengths):
    requests, tokens, heads, nope_width = q_nope.shape
    rope_width = q_rope.shape[3]
    width = w_uk.shape[2]
    rows = tokens * heads
    chips = tensor // 2
    factor = (nope_width + rope_width) ** -0.5 * math.log2(math.e)
    halves = math.gcd(requests, 2)
    half = requests // halves

    def move(x, chip, core):
        pairs = [(i, 2 * ((i // 2 + chip) % chips) + ((i % 2) ^ core)) for i in range(tensor)]
        return lax.ppermute(x, "tensor", pairs)

    def cross(x):
        return {d: move(x, d, 0) for d in range(1, chips)}

    def spread(x, crossed):
        found = {(0, 0): x, (0, 1): move(x, 0, 1)}
        for d in range(1, chips):
            found[d, 0] = crossed[d]
        for d in range(1, chips):
            found[d, 1] = move(crossed[d], 0, 1)
        return found

    own = (
        jnp.einsum("rthn,hnc->rthc", q_nope, w_uk, preferred_element_type=f32)
        .astype(bf16)
        .reshape(requests, rows, width)
    )
    rope_rows = q_rope.reshape(requests, rows, rope_width)
    own, rope_rows, scale_pool = lax.optimization_barrier((own, rope_rows, scale_pool))
    scales = spread(scale_pool, cross(scale_pool))
    ropes = spread(rope_rows, cross(rope_rows))
    query = spread(own, cross(own))
    table = jnp.stack(list(scales.values()))
    cache = prepare(0, requests, block_index, table, cache_latent, cache_rope)
    after = lengths
    back, own_parts = [], []
    for d in [*range(1, chips), 0]:
        pieces = halves if d == 0 else 1
        count = requests // pieces
        for h in range(pieces):
            oa, ob, la, lb = attend(
                h * count, count, lengths, query[d, 0], query[d, 1], ropes[d, 0], ropes[d, 1], *cache, after, tokens, factor
            )
            after = la
            ob, lb = move(ob, 0, 1), move(lb, 0, 1)
            if d == 0:
                own_parts.append(([oa, ob], [la, lb]))
            else:
                joined, level = weigh([oa, ob], [la, lb])
                level = move(level, -d, 0)
                back.append((move(joined.astype(bf16), -d, 0), level))
    attended = jnp.concatenate(
        [
            weigh(
                parts + [x[h * half : (h + 1) * half] for x, _ in back],
                levels + [y[h * half : (h + 1) * half] for _, y in back],
            )[0].astype(bf16)
            for h, (parts, levels) in enumerate(own_parts)
        ]
    )
    attended = attended.reshape(requests, tokens, heads, width)
    projected = jnp.einsum("rthc,hcv->rthv", attended, w_uv, preferred_element_type=f32)
    return projected.astype(bf16)


def solution(mesh):
    placed = (
        P("dp", None, "tensor", None),
        P("dp", None, "tensor", None),
        P("tensor", None, None),
        P("tensor", None, None),
        P("dp", "tensor", None),
        P("dp", None, "tensor"),
        P(None, ("dp", "tensor")),
        P("dp", "tensor"),
        P("dp"),
    )

    def body(*args):
        return local(mesh.shape["tensor"], *args)

    return jax.shard_map(
        body,
        mesh=mesh,
        in_specs=placed,
        out_specs=P("dp", None, "tensor", None),
        check_vma=False,
    )
```

```python
import functools
import math

import jax
import jax.numpy as jnp
from jax import lax
from jax.experimental import pallas as pl
from jax.experimental.pallas import tpu as pltpu
from jax.sharding import PartitionSpec as P


f32, bf16 = jnp.float32, jnp.bfloat16
masked_score = -1e30
VMEM = pl.BlockSpec(memory_space=pltpu.VMEM)
SMEM = pl.BlockSpec(memory_space=pltpu.SMEM)
HBM = pl.BlockSpec(memory_space=pltpu.HBM)


def prepare_kernel(
    first, pieces, index_ref, scale_ref, latent_hbm, rope_hbm, key_ref, turned_ref, latent, rope, latent_sem, rope_sem
):
    requests, span, width = latent.shape
    blocks = index_ref.shape[1]
    shards, groups, per = scale_ref.shape
    block = span // blocks
    lanes = width // (groups - 1)
    me = lax.axis_index("tensor")
    chips = shards // 2
    step = blocks // pieces

    def latent_copy(r, p):
        at = pl.ds(p * step * block, step * block)
        return pltpu.make_async_copy(
            latent_hbm.at[first + r, at], latent.at[r, at], latent_sem.at[r, p]
        )

    def rope_copy(r):
        return pltpu.make_async_copy(rope_hbm.at[first + r], rope.at[r], rope_sem.at[r])

    for r in range(requests):
        rope_copy(r).start()
        for p in range(pieces):
            latent_copy(r, p).start()

    for r in range(requests):
        rope_copy(r).wait()
        for p in range(pieces):
            latent_copy(r, p).wait()
            for b in range(p * step, (p + 1) * step):
                column = index_ref[first + r, b]
                owner, place = lax.div(column, per), lax.rem(column, per)
                turn = lax.rem(me // 2 - owner // 2 + chips, chips)
                other = (me - owner) & 1
                shard = jnp.where(turn == 0, other, turn + 1 + other * (chips - 1))
                at = pl.ds(b * block, block)
                for g in range(groups - 1):
                    part = pl.ds(g * lanes, lanes)
                    scaled = (latent[r, at, part].astype(f32) * scale_ref[shard, g, place]).astype(bf16)
                    key_ref[r, at, part] = scaled
                    turned_ref[r, part, at] = scaled.T
                turned_ref[r, pl.ds(width, rope.shape[1]), at] = (
                    rope[r, :, at].astype(f32) * scale_ref[shard, groups - 1, place]
                ).astype(bf16)


def prepare(first, requests, index, scales, latent, rope):
    span, width = latent.shape[1:]
    depth = rope.shape[1]
    pieces = 1
    return pl.pallas_call(
        functools.partial(prepare_kernel, first, pieces),
        in_specs=[SMEM, SMEM, HBM, HBM],
        out_specs=[VMEM, VMEM],
        out_shape=[
            jax.ShapeDtypeStruct((requests, span, width), bf16),
            jax.ShapeDtypeStruct((requests, width + depth, span), bf16),
        ],
        scratch_shapes=[
            pltpu.VMEM((requests, span, width), bf16),
            pltpu.VMEM((requests, depth, span), bf16),
            pltpu.SemaphoreType.DMA((requests, pieces)),
            pltpu.SemaphoreType.DMA((requests,)),
        ],
        compiler_params=pltpu.CompilerParams(vmem_limit_bytes=12 << 20),
        cost_estimate=pl.CostEstimate(flops=20_000_000, bytes_accessed=20_000_000, transcendentals=0),
        name="prepare",
    )(
        index,
        scales,
        pltpu.with_memory_space_constraint(latent, pltpu.HBM),
        pltpu.with_memory_space_constraint(rope, pltpu.HBM),
    )


def attend_kernel(
    first, tokens, factor, length_ref, qa_ref, qb_ref, ra_ref, rb_ref, key_ref, turned_ref, after_ref,
    oa_ref, ob_ref, la_ref, lb_ref,
):
    requests, _, rows = la_ref.shape
    span = key_ref.shape[1]
    heads = rows // tokens

    position = lax.broadcasted_iota(jnp.int32, (1, span), 1)

    def score(r):
        query = jnp.concatenate(
            [
                jnp.concatenate([qa_ref[first + r], ra_ref[(first + r) * rows : (first + r + 1) * rows]], axis=1),
                jnp.concatenate([qb_ref[first + r], rb_ref[(first + r) * rows : (first + r + 1) * rows]], axis=1),
            ],
            axis=0,
        )
        return jnp.dot(query, turned_ref[first + r], preferred_element_type=f32)

    ahead = score(0)
    for r in range(requests):
        scores = ahead * factor
        if r + 1 < requests:
            ahead = score(r + 1)
        limit = length_ref[first + r] - tokens - lax.axis_index("tensor") * span
        bias = [
            jnp.where(position <= limit + t, 0.0, masked_score).astype(f32) for t in range(tokens)
        ]
        scores = jnp.concatenate(
            [scores[k * heads : (k + 1) * heads] + bias[k % tokens] for k in range(2 * tokens)], axis=0
        )
        peak = jnp.max(scores, axis=1, keepdims=True)
        weights = jnp.exp2(scores - peak)
        total = jnp.sum(weights, axis=1, keepdims=True)
        mixture = jnp.dot(weights.astype(bf16), key_ref[first + r], preferred_element_type=f32)
        mixture = (mixture * (1.0 / total)).astype(bf16)
        oa_ref[r] = mixture[:rows]
        ob_ref[r] = mixture[rows:]
        level = jnp.broadcast_to(peak + jnp.log2(total), (2 * rows, 128)).T[:1]
        la_ref[r] = level[:, :rows]
        lb_ref[r] = level[:, rows:]


def attend(first, requests, lengths, qa, qb, ra, rb, key, turned, after, tokens, factor):
    _, rows, width = qa.shape
    span = key.shape[1]
    mixed = jax.ShapeDtypeStruct((requests, rows, width), bf16)
    level = jax.ShapeDtypeStruct((requests, 1, rows), f32)
    return pl.pallas_call(
        functools.partial(attend_kernel, first, tokens, factor),
        in_specs=[SMEM] + [VMEM] * 6 + [pl.BlockSpec(memory_space=pl.ANY)],
        out_specs=[VMEM] * 4,
        out_shape=[mixed, mixed, level, level],
        compiler_params=pltpu.CompilerParams(vmem_limit_bytes=8 << 20),
        cost_estimate=pl.CostEstimate(
            flops=4 * requests * rows * span * (2 * width + 64),
            bytes_accessed=requests * span * width * 2,
            transcendentals=2 * requests * rows * span,
        ),
        name="attend",
    )(lengths, qa, qb, ra, rb, key, turned, after)


def weigh(parts, levels):
    top = functools.reduce(jnp.maximum, levels)
    shares = [jnp.exp2(level - top) for level in levels]
    total = functools.reduce(jnp.add, shares)
    columns = [jnp.swapaxes(share / total, 1, 2) for share in shares]
    joined = functools.reduce(
        jnp.add, [part.astype(f32) * column for part, column in zip(parts, columns)]
    )
    return joined, top + jnp.log2(total)


def local(tensor, q_nope, q_rope, w_uk, w_uv, cache_latent, cache_rope, scale_pool, block_index, lengths):
    requests, tokens, heads, nope_width = q_nope.shape
    rope_width = q_rope.shape[3]
    width = w_uk.shape[2]
    rows = tokens * heads
    chips = tensor // 2
    factor = (nope_width + rope_width) ** -0.5 * math.log2(math.e)

    def move(x, chip, core):
        pairs = [(i, 2 * ((i // 2 + chip) % chips) + ((i % 2) ^ core)) for i in range(tensor)]
        return lax.ppermute(x, "tensor", pairs)

    def cross(x):
        return {d: move(x, d, 0) for d in range(1, chips)}

    def spread(x, crossed):
        found = {(0, 0): x, (0, 1): move(x, 0, 1)}
        for d in range(1, chips):
            found[d, 0] = crossed[d]
        for d in range(1, chips):
            found[d, 1] = move(crossed[d], 0, 1)
        return found

    own = (
        jnp.einsum("rthn,hnc->rthc", q_nope, w_uk, preferred_element_type=f32)
        .astype(bf16)
        .reshape(requests, rows, width)
    )
    terms = []
    rest = scale_pool
    for _ in range(3):
        terms.append(lax.reduce_precision(rest, 8, 7))
        rest = rest - terms[-1]
    groups, per = scale_pool.shape
    terms = jnp.concatenate(terms).astype(bf16)
    if per != rope_width:
        terms = terms.reshape(-1)
        terms = jnp.pad(terms, (0, -terms.size % rope_width)).reshape(-1, rope_width)
    count = requests * rows
    small = jnp.concatenate([q_rope.reshape(count, rope_width), terms])
    small = jnp.pad(small, ((0, -small.shape[0] % 16), (0, 0)))
    smalls = spread(small, cross(small))
    query = spread(own, cross(own))

    def scales_of(x):
        coded = x[count : count + terms.shape[0]].astype(f32)
        if per != rope_width:
            coded = coded.reshape(-1)[: 3 * groups * per].reshape(3 * groups, per)
        return coded[:groups] + coded[groups : 2 * groups] + coded[2 * groups :]

    table = jnp.stack([scales_of(x) for x in smalls.values()])
    cache = prepare(0, requests, block_index, table, cache_latent, cache_rope)
    after = lengths
    parts, levels = [], []
    for d in [*range(1, chips), 0]:
        oa, ob, la, lb = attend(
            0, requests, lengths, query[d, 0], query[d, 1], smalls[d, 0], smalls[d, 1], *cache, after, tokens, factor
        )
        after = la
        ob, lb = move(ob, 0, 1), move(lb, 0, 1)
        if d == 0:
            parts += [oa, ob]
            levels += [la, lb]
        else:
            joined, level = weigh([oa, ob], [la, lb])
            levels.append(move(level, -d, 0))
            parts.append(move(joined.astype(bf16), -d, 0))
    attended = weigh(parts, levels)[0].astype(bf16)
    attended = attended.reshape(requests, tokens, heads, width)
    projected = jnp.einsum("rthc,hcv->rthv", attended, w_uv, preferred_element_type=f32)
    return projected.astype(bf16)


def solution(mesh):
    placed = (
        P("dp", None, "tensor", None),
        P("dp", None, "tensor", None),
        P("tensor", None, None),
        P("tensor", None, None),
        P("dp", "tensor", None),
        P("dp", None, "tensor"),
        P(None, ("dp", "tensor")),
        P("dp", "tensor"),
        P("dp"),
    )

    def body(*args):
        return local(mesh.shape["tensor"], *args)

    return jax.shard_map(
        body,
        mesh=mesh,
        in_specs=placed,
        out_specs=P("dp", None, "tensor", None),
        check_vma=False,
    )
```

```python
import functools
import math

import jax
import jax.numpy as jnp
from jax import lax
from jax.experimental import pallas as pl
from jax.experimental.pallas import tpu as pltpu
from jax.sharding import PartitionSpec as P


f32, bf16 = jnp.float32, jnp.bfloat16
masked_score = -1e30
VMEM = pl.BlockSpec(memory_space=pltpu.VMEM)
SMEM = pl.BlockSpec(memory_space=pltpu.SMEM)
HBM = pl.BlockSpec(memory_space=pltpu.HBM)


def prepare_kernel(
    first, pieces, index_ref, scale_ref, latent_hbm, rope_hbm, key_ref, turned_ref, latent, rope, latent_sem, rope_sem
):
    requests, span, width = latent.shape
    blocks = index_ref.shape[1]
    shards, groups, per = scale_ref.shape
    block = span // blocks
    lanes = width // (groups - 1)
    me = lax.axis_index("tensor")
    chips = shards // 2
    step = blocks // pieces

    def latent_copy(r, p):
        at = pl.ds(p * step * block, step * block)
        return pltpu.make_async_copy(
            latent_hbm.at[first + r, at], latent.at[r, at], latent_sem.at[r, p]
        )

    def rope_copy(r):
        return pltpu.make_async_copy(rope_hbm.at[first + r], rope.at[r], rope_sem.at[r])

    for r in range(requests):
        rope_copy(r).start()
        for p in range(pieces):
            latent_copy(r, p).start()

    for r in range(requests):
        rope_copy(r).wait()
        for p in range(pieces):
            latent_copy(r, p).wait()
            for b in range(p * step, (p + 1) * step):
                column = index_ref[first + r, b]
                owner, place = lax.div(column, per), lax.rem(column, per)
                turn = lax.rem(me // 2 - owner // 2 + chips, chips)
                other = (me - owner) & 1
                shard = jnp.where(turn == 0, other, turn + 1 + other * (chips - 1))
                at = pl.ds(b * block, block)
                for g in range(groups - 1):
                    part = pl.ds(g * lanes, lanes)
                    scaled = (latent[r, at, part].astype(f32) * scale_ref[shard, g, place]).astype(bf16)
                    key_ref[r, at, part] = scaled
                    turned_ref[r, part, at] = scaled.T
                turned_ref[r, pl.ds(width, rope.shape[1]), at] = (
                    rope[r, :, at].astype(f32) * scale_ref[shard, groups - 1, place]
                ).astype(bf16)


def prepare(first, requests, index, scales, latent, rope):
    span, width = latent.shape[1:]
    depth = rope.shape[1]
    pieces = 1
    return pl.pallas_call(
        functools.partial(prepare_kernel, first, pieces),
        in_specs=[SMEM, SMEM, HBM, HBM],
        out_specs=[VMEM, VMEM],
        out_shape=[
            jax.ShapeDtypeStruct((requests, span, width), bf16),
            jax.ShapeDtypeStruct((requests, width + depth, span), bf16),
        ],
        scratch_shapes=[
            pltpu.VMEM((requests, span, width), bf16),
            pltpu.VMEM((requests, depth, span), bf16),
            pltpu.SemaphoreType.DMA((requests, pieces)),
            pltpu.SemaphoreType.DMA((requests,)),
        ],
        compiler_params=pltpu.CompilerParams(vmem_limit_bytes=12 << 20),
        cost_estimate=pl.CostEstimate(flops=20_000_000, bytes_accessed=20_000_000, transcendentals=0),
        name="prepare",
    )(
        index,
        scales,
        pltpu.with_memory_space_constraint(latent, pltpu.HBM),
        pltpu.with_memory_space_constraint(rope, pltpu.HBM),
    )


def attend_kernel(
    first, tokens, factor, length_ref, qa_ref, qb_ref, ra_ref, rb_ref, key_ref, turned_ref, after_ref,
    oa_ref, ob_ref, la_ref, lb_ref,
):
    requests, _, rows = la_ref.shape
    span = key_ref.shape[1]
    heads = rows // tokens

    position = lax.broadcasted_iota(jnp.int32, (1, span), 1)

    def score(r):
        query = jnp.concatenate(
            [
                jnp.concatenate([qa_ref[r], ra_ref[first + r]], axis=1),
                jnp.concatenate([qb_ref[r], rb_ref[first + r]], axis=1),
            ],
            axis=0,
        )
        return jnp.dot(query, turned_ref[first + r], preferred_element_type=f32)

    ahead = score(0)
    for r in range(requests):
        scores = ahead * factor
        if r + 1 < requests:
            ahead = score(r + 1)
        limit = length_ref[first + r] - tokens - lax.axis_index("tensor") * span
        bias = [
            jnp.where(position <= limit + t, 0.0, masked_score).astype(f32) for t in range(tokens)
        ]
        scores = jnp.concatenate(
            [scores[k * heads : (k + 1) * heads] + bias[k % tokens] for k in range(2 * tokens)], axis=0
        )
        peak = jnp.max(scores, axis=1, keepdims=True)
        weights = jnp.exp2(scores - peak)
        total = jnp.sum(weights, axis=1, keepdims=True)
        mixture = jnp.dot(weights.astype(bf16), key_ref[first + r], preferred_element_type=f32)
        mixture = (mixture * (1.0 / total)).astype(bf16)
        oa_ref[r] = mixture[:rows]
        ob_ref[r] = mixture[rows:]
        level = jnp.broadcast_to(peak + jnp.log2(total), (2 * rows, 128)).T[:1]
        la_ref[r] = level[:, :rows]
        lb_ref[r] = level[:, rows:]


def attend(first, lengths, qa, qb, ra, rb, key, turned, after, tokens, factor):
    requests, rows, width = qa.shape
    span = key.shape[1]
    mixed = jax.ShapeDtypeStruct((requests, rows, width), bf16)
    level = jax.ShapeDtypeStruct((requests, 1, rows), f32)
    return pl.pallas_call(
        functools.partial(attend_kernel, first, tokens, factor),
        in_specs=[SMEM] + [VMEM] * 6 + [pl.BlockSpec(memory_space=pl.ANY)],
        out_specs=[VMEM] * 4,
        out_shape=[mixed, mixed, level, level],
        compiler_params=pltpu.CompilerParams(vmem_limit_bytes=8 << 20),
        cost_estimate=pl.CostEstimate(
            flops=4 * requests * rows * span * (2 * width + 64),
            bytes_accessed=requests * span * width * 2,
            transcendentals=2 * requests * rows * span,
        ),
        name="attend",
    )(lengths, qa, qb, ra, rb, key, turned, after)


def weigh(parts, levels):
    top = functools.reduce(jnp.maximum, levels)
    shares = [jnp.exp2(level - top) for level in levels]
    total = functools.reduce(jnp.add, shares)
    columns = [jnp.swapaxes(share / total, 1, 2) for share in shares]
    joined = functools.reduce(
        jnp.add, [part.astype(f32) * column for part, column in zip(parts, columns)]
    )
    return joined, top + jnp.log2(total)


def local(tensor, q_nope, q_rope, w_uk, w_uv, cache_latent, cache_rope, scale_pool, block_index, lengths):
    requests, tokens, heads, nope_width = q_nope.shape
    rope_width = q_rope.shape[3]
    width = w_uk.shape[2]
    rows = tokens * heads
    chips = tensor // 2
    half = requests // 2 if chips == 2 and requests % 2 == 0 else requests
    factor = (nope_width + rope_width) ** -0.5 * math.log2(math.e)

    def move(x, chip, core):
        pairs = [(i, 2 * ((i // 2 + chip) % chips) + ((i % 2) ^ core)) for i in range(tensor)]
        return lax.ppermute(x, "tensor", pairs)

    def cross(x):
        return {d: move(x, d, 0) for d in range(1, chips)}

    def spread(x, crossed):
        found = {(0, 0): x, (0, 1): move(x, 0, 1)}
        for d in range(1, chips):
            found[d, 0] = crossed[d]
        for d in range(1, chips):
            found[d, 1] = move(crossed[d], 0, 1)
        return found

    own = (
        jnp.einsum("rthn,hnc->rthc", q_nope, w_uk, preferred_element_type=f32)
        .astype(bf16)
        .reshape(requests, rows, width)
    )
    rope_rows = q_rope.reshape(requests, rows, rope_width)
    scales = spread(scale_pool, cross(scale_pool))
    ropes = spread(rope_rows, cross(rope_rows))
    halves = [own[h * half : (h + 1) * half] for h in range(requests // half)]
    crossed = [cross(x) for x in halves]
    query = [{(d, 0): crossed[h][d] for d in range(1, chips)} for h in range(len(halves))]
    for h in range(len(halves)):
        for d in range(1, chips):
            query[h][d, 1] = move(crossed[h][d], 0, 1)
    partner = move(own, 0, 1)
    table = jnp.stack(list(scales.values()))
    cache = prepare(0, requests, block_index, table, cache_latent, cache_rope)
    after = lengths
    parts, levels = [], []
    for d in range(1, chips):
        joined, level = [], []
        for h in range(len(halves)):
            oa, ob, la, lb = attend(
                h * half, lengths, query[h][d, 0], query[h][d, 1], ropes[d, 0], ropes[d, 1], *cache, after, tokens, factor
            )
            after = la
            ob, lb = move(ob, 0, 1), move(lb, 0, 1)
            both = weigh([oa, ob], [la, lb])
            joined.append(both[0].astype(bf16))
            level.append(both[1])
        levels.append(move(jnp.concatenate(level), -d, 0))
        parts.append(move(jnp.concatenate(joined), -d, 0))
    oa, ob, la, lb = attend(
        0, lengths, own, partner, ropes[0, 0], ropes[0, 1], *cache, after, tokens, factor
    )
    parts += [oa, move(ob, 0, 1)]
    levels += [la, move(lb, 0, 1)]
    attended = weigh(parts, levels)[0].astype(bf16)
    attended = attended.reshape(requests, tokens, heads, width)
    projected = jnp.einsum("rthc,hcv->rthv", attended, w_uv, preferred_element_type=f32)
    return projected.astype(bf16)


def solution(mesh):
    placed = (
        P("dp", None, "tensor", None),
        P("dp", None, "tensor", None),
        P("tensor", None, None),
        P("tensor", None, None),
        P("dp", "tensor", None),
        P("dp", None, "tensor"),
        P(None, ("dp", "tensor")),
        P("dp", "tensor"),
        P("dp"),
    )

    def body(*args):
        return local(mesh.shape["tensor"], *args)

    return jax.shard_map(
        body,
        mesh=mesh,
        in_specs=placed,
        out_specs=P("dp", None, "tensor", None),
        check_vma=False,
    )
```

```python
import functools
import math

import jax
import jax.numpy as jnp
from jax import lax
from jax.experimental import pallas as pl
from jax.experimental.pallas import tpu as pltpu
from jax.sharding import PartitionSpec as P


f32, bf16 = jnp.float32, jnp.bfloat16
masked_score = -1e30
VMEM = pl.BlockSpec(memory_space=pltpu.VMEM)
SMEM = pl.BlockSpec(memory_space=pltpu.SMEM)
HBM = pl.BlockSpec(memory_space=pltpu.HBM)


def prepare_kernel(
    first, pieces, index_ref, scale_ref, latent_hbm, rope_hbm, key_ref, turned_ref, latent, rope, latent_sem, rope_sem
):
    requests, span, width = latent.shape
    blocks = index_ref.shape[1]
    shards, groups, per = scale_ref.shape
    block = span // blocks
    lanes = width // (groups - 1)
    me = lax.axis_index("tensor")
    chips = shards // 2
    step = blocks // pieces

    def latent_copy(r, p):
        at = pl.ds(p * step * block, step * block)
        return pltpu.make_async_copy(
            latent_hbm.at[first + r, at], latent.at[r, at], latent_sem.at[r, p]
        )

    def rope_copy(r):
        return pltpu.make_async_copy(rope_hbm.at[first + r], rope.at[r], rope_sem.at[r])

    for r in range(requests):
        rope_copy(r).start()
        for p in range(pieces):
            latent_copy(r, p).start()

    for r in range(requests):
        rope_copy(r).wait()
        for p in range(pieces):
            latent_copy(r, p).wait()
            for b in range(p * step, (p + 1) * step):
                column = index_ref[first + r, b]
                owner, place = lax.div(column, per), lax.rem(column, per)
                turn = lax.rem(me // 2 - owner // 2 + chips, chips)
                other = (me - owner) & 1
                shard = jnp.where(turn == 0, other, turn + 1 + other * (chips - 1))
                at = pl.ds(b * block, block)
                for g in range(groups - 1):
                    part = pl.ds(g * lanes, lanes)
                    scaled = (latent[r, at, part].astype(f32) * scale_ref[shard, g, place]).astype(bf16)
                    key_ref[r, at, part] = scaled
                    turned_ref[r, part, at] = scaled.T
                turned_ref[r, pl.ds(width, rope.shape[1]), at] = (
                    rope[r, :, at].astype(f32) * scale_ref[shard, groups - 1, place]
                ).astype(bf16)


def prepare(first, requests, index, scales, latent, rope):
    span, width = latent.shape[1:]
    depth = rope.shape[1]
    pieces = 1
    return pl.pallas_call(
        functools.partial(prepare_kernel, first, pieces),
        in_specs=[SMEM, SMEM, HBM, HBM],
        out_specs=[VMEM, VMEM],
        out_shape=[
            jax.ShapeDtypeStruct((requests, span, width), bf16),
            jax.ShapeDtypeStruct((requests, width + depth, span), bf16),
        ],
        scratch_shapes=[
            pltpu.VMEM((requests, span, width), bf16),
            pltpu.VMEM((requests, depth, span), bf16),
            pltpu.SemaphoreType.DMA((requests, pieces)),
            pltpu.SemaphoreType.DMA((requests,)),
        ],
        compiler_params=pltpu.CompilerParams(vmem_limit_bytes=12 << 20),
        cost_estimate=pl.CostEstimate(flops=20_000_000, bytes_accessed=20_000_000, transcendentals=0),
        name="prepare",
    )(
        index,
        scales,
        pltpu.with_memory_space_constraint(latent, pltpu.HBM),
        pltpu.with_memory_space_constraint(rope, pltpu.HBM),
    )


def attend_kernel(
    first, tokens, factor, length_ref, qa_ref, qb_ref, ra_ref, rb_ref, key_ref, turned_ref, after_ref,
    oa_ref, ob_ref, la_ref, lb_ref,
):
    requests, _, rows = la_ref.shape
    span = key_ref.shape[1]
    heads = rows // tokens

    position = lax.broadcasted_iota(jnp.int32, (1, span), 1)

    def score(r):
        query = jnp.concatenate(
            [
                jnp.concatenate([qa_ref[r], ra_ref[first + r]], axis=1),
                jnp.concatenate([qb_ref[r], rb_ref[first + r]], axis=1),
            ],
            axis=0,
        )
        return jnp.dot(query, turned_ref[first + r], preferred_element_type=f32)

    ahead = score(0)
    for r in range(requests):
        scores = ahead * factor
        if r + 1 < requests:
            ahead = score(r + 1)
        limit = length_ref[first + r] - tokens - lax.axis_index("tensor") * span
        bias = [
            jnp.where(position <= limit + t, 0.0, masked_score).astype(f32) for t in range(tokens)
        ]
        scores = jnp.concatenate(
            [scores[k * heads : (k + 1) * heads] + bias[k % tokens] for k in range(2 * tokens)], axis=0
        )
        peak = jnp.max(scores, axis=1, keepdims=True)
        weights = jnp.exp2(scores - peak)
        total = jnp.sum(weights, axis=1, keepdims=True)
        mixture = jnp.dot(weights.astype(bf16), key_ref[first + r], preferred_element_type=f32)
        mixture = (mixture * (1.0 / total)).astype(bf16)
        oa_ref[r] = mixture[:rows]
        ob_ref[r] = mixture[rows:]
        level = jnp.broadcast_to(peak + jnp.log2(total), (2 * rows, 128)).T[:1]
        la_ref[r] = level[:, :rows]
        lb_ref[r] = level[:, rows:]


def attend(first, lengths, qa, qb, ra, rb, key, turned, after, tokens, factor):
    requests, rows, width = qa.shape
    span = key.shape[1]
    mixed = jax.ShapeDtypeStruct((requests, rows, width), bf16)
    level = jax.ShapeDtypeStruct((requests, 1, rows), f32)
    return pl.pallas_call(
        functools.partial(attend_kernel, first, tokens, factor),
        in_specs=[SMEM] + [VMEM] * 6 + [pl.BlockSpec(memory_space=pl.ANY)],
        out_specs=[VMEM] * 4,
        out_shape=[mixed, mixed, level, level],
        compiler_params=pltpu.CompilerParams(vmem_limit_bytes=8 << 20),
        cost_estimate=pl.CostEstimate(
            flops=4 * requests * rows * span * (2 * width + 64),
            bytes_accessed=requests * span * width * 2,
            transcendentals=2 * requests * rows * span,
        ),
        name="attend",
    )(lengths, qa, qb, ra, rb, key, turned, after)


def weigh(parts, levels):
    top = functools.reduce(jnp.maximum, levels)
    shares = [jnp.exp2(level - top) for level in levels]
    total = functools.reduce(jnp.add, shares)
    columns = [jnp.swapaxes(share / total, 1, 2) for share in shares]
    joined = functools.reduce(
        jnp.add, [part.astype(f32) * column for part, column in zip(parts, columns)]
    )
    return joined, top + jnp.log2(total)


def local(tensor, q_nope, q_rope, w_uk, w_uv, cache_latent, cache_rope, scale_pool, block_index, lengths):
    requests, tokens, heads, nope_width = q_nope.shape
    rope_width = q_rope.shape[3]
    width = w_uk.shape[2]
    rows = tokens * heads
    chips = tensor // 2
    half = requests // 2 if chips == 2 and requests % 2 == 0 else requests
    factor = (nope_width + rope_width) ** -0.5 * math.log2(math.e)

    def move(x, chip, core):
        pairs = [(i, 2 * ((i // 2 + chip) % chips) + ((i % 2) ^ core)) for i in range(tensor)]
        return lax.ppermute(x, "tensor", pairs)

    def cross(x):
        return {d: move(x, d, 0) for d in range(1, chips)}

    def spread(x, crossed):
        found = {(0, 0): x, (0, 1): move(x, 0, 1)}
        for d in range(1, chips):
            found[d, 0] = crossed[d]
        for d in range(1, chips):
            found[d, 1] = move(crossed[d], 0, 1)
        return found

    own = (
        jnp.einsum("rthn,hnc->rthc", q_nope, w_uk, preferred_element_type=f32)
        .astype(bf16)
        .reshape(requests, rows, width)
    )
    rope_rows = q_rope.reshape(requests, rows, rope_width)
    scales = spread(scale_pool, cross(scale_pool))
    ropes = spread(rope_rows, cross(rope_rows))
    halves = [own[h * half : (h + 1) * half] for h in range(requests // half)]
    crossed = [cross(x) for x in halves]
    query = [{(d, 0): crossed[h][d] for d in range(1, chips)} for h in range(len(halves))]
    for h in range(len(halves)):
        for d in range(1, chips):
            query[h][d, 1] = move(crossed[h][d], 0, 1)
    partner = move(own, 0, 1)
    table = jnp.stack(list(scales.values()))
    cache = prepare(0, requests, block_index, table, cache_latent, cache_rope)
    after = lengths
    parts, levels = [], []
    for d in range(1, chips):
        joined, level = [], []
        for h in range(len(halves)):
            oa, ob, la, lb = attend(
                h * half, lengths, query[h][d, 0], query[h][d, 1], ropes[d, 0], ropes[d, 1], *cache, after, tokens, factor
            )
            after = la
            ob, lb = move(ob, 0, 1), move(lb, 0, 1)
            both = weigh([oa, ob], [la, lb])
            both = both[0].astype(bf16), both[1]
            level.append(move(both[1], -d, 0))
            joined.append(move(both[0], -d, 0))
        levels.append(jnp.concatenate(level))
        parts.append(jnp.concatenate(joined))
    oa, ob, la, lb = attend(
        0, lengths, own, partner, ropes[0, 0], ropes[0, 1], *cache, after, tokens, factor
    )
    parts += [oa, move(ob, 0, 1)]
    levels += [la, move(lb, 0, 1)]
    attended = weigh(parts, levels)[0].astype(bf16)
    attended = attended.reshape(requests, tokens, heads, width)
    projected = jnp.einsum("rthc,hcv->rthv", attended, w_uv, preferred_element_type=f32)
    return projected.astype(bf16)


def solution(mesh):
    placed = (
        P("dp", None, "tensor", None),
        P("dp", None, "tensor", None),
        P("tensor", None, None),
        P("tensor", None, None),
        P("dp", "tensor", None),
        P("dp", None, "tensor"),
        P(None, ("dp", "tensor")),
        P("dp", "tensor"),
        P("dp"),
    )

    def body(*args):
        return local(mesh.shape["tensor"], *args)

    return jax.shard_map(
        body,
        mesh=mesh,
        in_specs=placed,
        out_specs=P("dp", None, "tensor", None),
        check_vma=False,
    )
```

```python
import functools
import math

import jax
import jax.numpy as jnp
from jax import lax
from jax.experimental import pallas as pl
from jax.experimental.pallas import tpu as pltpu
from jax.sharding import PartitionSpec as P


f32, bf16 = jnp.float32, jnp.bfloat16
masked_score = -1e30
VMEM = pl.BlockSpec(memory_space=pltpu.VMEM)
SMEM = pl.BlockSpec(memory_space=pltpu.SMEM)
HBM = pl.BlockSpec(memory_space=pltpu.HBM)


def prepare_kernel(
    first, pieces, index_ref, scale_ref, latent_hbm, rope_hbm, key_ref, turned_ref, latent, rope, latent_sem, rope_sem
):
    requests, span, width = latent.shape
    blocks = index_ref.shape[1]
    shards, groups, per = scale_ref.shape
    block = span // blocks
    lanes = width // (groups - 1)
    me = lax.axis_index("tensor")
    chips = shards // 2
    step = blocks // pieces

    def latent_copy(r, p):
        at = pl.ds(p * step * block, step * block)
        return pltpu.make_async_copy(
            latent_hbm.at[first + r, at], latent.at[r, at], latent_sem.at[r, p]
        )

    def rope_copy(r):
        return pltpu.make_async_copy(rope_hbm.at[first + r], rope.at[r], rope_sem.at[r])

    for r in range(requests):
        rope_copy(r).start()
        for p in range(pieces):
            latent_copy(r, p).start()

    for r in range(requests):
        rope_copy(r).wait()
        for p in range(pieces):
            latent_copy(r, p).wait()
            for b in range(p * step, (p + 1) * step):
                column = index_ref[first + r, b]
                owner, place = lax.div(column, per), lax.rem(column, per)
                turn = lax.rem(me // 2 - owner // 2 + chips, chips)
                other = (me - owner) & 1
                shard = jnp.where(turn == 0, other, turn + 1 + other * (chips - 1))
                at = pl.ds(b * block, block)
                for g in range(groups - 1):
                    part = pl.ds(g * lanes, lanes)
                    scaled = (latent[r, at, part].astype(f32) * scale_ref[shard, g, place]).astype(bf16)
                    key_ref[r, at, part] = scaled
                    turned_ref[r, part, at] = scaled.T
                turned_ref[r, pl.ds(width, rope.shape[1]), at] = (
                    rope[r, :, at].astype(f32) * scale_ref[shard, groups - 1, place]
                ).astype(bf16)


def prepare(first, requests, index, scales, latent, rope):
    span, width = latent.shape[1:]
    depth = rope.shape[1]
    pieces = 1
    return pl.pallas_call(
        functools.partial(prepare_kernel, first, pieces),
        in_specs=[SMEM, SMEM, HBM, HBM],
        out_specs=[VMEM, VMEM],
        out_shape=[
            jax.ShapeDtypeStruct((requests, span, width), bf16),
            jax.ShapeDtypeStruct((requests, width + depth, span), bf16),
        ],
        scratch_shapes=[
            pltpu.VMEM((requests, span, width), bf16),
            pltpu.VMEM((requests, depth, span), bf16),
            pltpu.SemaphoreType.DMA((requests, pieces)),
            pltpu.SemaphoreType.DMA((requests,)),
        ],
        compiler_params=pltpu.CompilerParams(vmem_limit_bytes=12 << 20),
        cost_estimate=pl.CostEstimate(flops=20_000_000, bytes_accessed=20_000_000, transcendentals=0),
        name="prepare",
    )(
        index,
        scales,
        pltpu.with_memory_space_constraint(latent, pltpu.HBM),
        pltpu.with_memory_space_constraint(rope, pltpu.HBM),
    )


def attend_kernel(
    first, tokens, factor, length_ref, qa_ref, qb_ref, ra_ref, rb_ref, key_ref, turned_ref, after_ref,
    oa_ref, ob_ref, la_ref, lb_ref,
):
    requests, _, rows = la_ref.shape
    span = key_ref.shape[1]
    heads = rows // tokens

    position = lax.broadcasted_iota(jnp.int32, (1, span), 1)

    def score(r):
        query = jnp.concatenate(
            [
                jnp.concatenate([qa_ref[r], ra_ref[first + r]], axis=1),
                jnp.concatenate([qb_ref[r], rb_ref[first + r]], axis=1),
            ],
            axis=0,
        )
        return jnp.dot(query, turned_ref[first + r], preferred_element_type=f32)

    ahead = score(0)
    for r in range(requests):
        scores = ahead * factor
        if r + 1 < requests:
            ahead = score(r + 1)
        limit = length_ref[first + r] - tokens - lax.axis_index("tensor") * span
        bias = [
            jnp.where(position <= limit + t, 0.0, masked_score).astype(f32) for t in range(tokens)
        ]
        scores = jnp.concatenate(
            [scores[k * heads : (k + 1) * heads] + bias[k % tokens] for k in range(2 * tokens)], axis=0
        )
        peak = jnp.max(scores, axis=1, keepdims=True)
        weights = jnp.exp2(scores - peak)
        total = jnp.sum(weights, axis=1, keepdims=True)
        mixture = jnp.dot(weights.astype(bf16), key_ref[first + r], preferred_element_type=f32)
        mixture = (mixture * (1.0 / total)).astype(bf16)
        oa_ref[r] = mixture[:rows]
        ob_ref[r] = mixture[rows:]
        level = jnp.broadcast_to(peak + jnp.log2(total), (2 * rows, 128)).T[:1]
        la_ref[r] = level[:, :rows]
        lb_ref[r] = level[:, rows:]


def attend(first, lengths, qa, qb, ra, rb, key, turned, after, tokens, factor):
    requests, rows, width = qa.shape
    span = key.shape[1]
    mixed = jax.ShapeDtypeStruct((requests, rows, width), bf16)
    level = jax.ShapeDtypeStruct((requests, 1, rows), f32)
    return pl.pallas_call(
        functools.partial(attend_kernel, first, tokens, factor),
        in_specs=[SMEM] + [VMEM] * 6 + [pl.BlockSpec(memory_space=pl.ANY)],
        out_specs=[VMEM] * 4,
        out_shape=[mixed, mixed, level, level],
        compiler_params=pltpu.CompilerParams(vmem_limit_bytes=8 << 20),
        cost_estimate=pl.CostEstimate(
            flops=4 * requests * rows * span * (2 * width + 64),
            bytes_accessed=requests * span * width * 2,
            transcendentals=2 * requests * rows * span,
        ),
        name="attend",
    )(lengths, qa, qb, ra, rb, key, turned, after)


def joined(parts, levels):
    rows, width = parts[0].shape
    top = functools.reduce(jnp.maximum, levels)
    shares = [jnp.exp2(level - top) for level in levels]
    total = functools.reduce(jnp.add, shares)
    mixed = None
    for part, share in zip(parts, shares):
        row = share / total
        if rows < 128:
            row = jnp.concatenate([row, jnp.zeros((1, 128 - rows), f32)], axis=1)
        column = jnp.broadcast_to(row, (128, row.shape[1])).T[:rows]
        term = part.astype(f32) * jnp.concatenate([column] * (width // 128), axis=1)
        mixed = term if mixed is None else mixed + term
    return mixed.astype(bf16), top + jnp.log2(total)


def weigh_kernel(oa_ref, ob_ref, la_ref, lb_ref, out_ref):
    requests, rows, width = oa_ref.shape
    levels = []
    for r in range(requests):
        mixed, level = joined([oa_ref[r], ob_ref[r]], [la_ref[r], lb_ref[r]])
        out_ref[r * rows : (r + 1) * rows] = mixed
        levels.append(level)
    rest = jnp.concatenate(levels, axis=1)
    count = requests * rows
    terms = []
    for _ in range(3):
        terms.append(rest.astype(bf16).astype(f32))
        rest = rest - terms[-1]
    terms = jnp.concatenate(terms + [jnp.zeros((5, count), f32)], axis=0)
    if count < width:
        terms = jnp.concatenate([terms, jnp.zeros((8, width - count), f32)], axis=1)
    out_ref[count:] = terms.astype(bf16)


def weigh(oa, ob, la, lb):
    requests, rows, width = oa.shape
    return pl.pallas_call(
        weigh_kernel,
        in_specs=[VMEM] * 4,
        out_specs=VMEM,
        out_shape=jax.ShapeDtypeStruct((requests * rows + 8, width), bf16),
        compiler_params=pltpu.CompilerParams(vmem_limit_bytes=6 << 20),
        cost_estimate=pl.CostEstimate(flops=200_000, bytes_accessed=500_000, transcendentals=1000),
        name="weigh",
    )(oa, ob, la, lb)


def finish_kernel(half, oa_ref, ob_ref, la_ref, lb_ref, *refs):
    out_ref, backs = refs[-1], refs[:-1]
    requests, rows, _ = oa_ref.shape
    count = half * rows
    pieces = requests // half
    levels = []
    for back in backs:
        terms = back[count : count + 8].astype(f32)
        levels.append((terms[0:1] + terms[1:2]) + terms[2:3])
    for r in range(requests):
        h, i = divmod(r, half)
        at = slice(i * rows, (i + 1) * rows)
        out_ref[r] = joined(
            [oa_ref[r], ob_ref[r]] + [back[at] for back in backs[h::pieces]],
            [la_ref[r], lb_ref[r]] + [level[:, at] for level in levels[h::pieces]],
        )[0]


def finish(half, oa, ob, la, lb, backs):
    return pl.pallas_call(
        functools.partial(finish_kernel, half),
        in_specs=[VMEM] * (4 + len(backs)),
        out_specs=VMEM,
        out_shape=jax.ShapeDtypeStruct(oa.shape, bf16),
        compiler_params=pltpu.CompilerParams(vmem_limit_bytes=6 << 20),
        cost_estimate=pl.CostEstimate(flops=500_000, bytes_accessed=1_000_000, transcendentals=2000),
        name="finish",
    )(oa, ob, la, lb, *backs)


def local(tensor, q_nope, q_rope, w_uk, w_uv, cache_latent, cache_rope, scale_pool, block_index, lengths):
    requests, tokens, heads, nope_width = q_nope.shape
    rope_width = q_rope.shape[3]
    width = w_uk.shape[2]
    rows = tokens * heads
    chips = tensor // 2
    half = requests // 2 if chips == 2 and requests % 2 == 0 else requests
    factor = (nope_width + rope_width) ** -0.5 * math.log2(math.e)

    def move(x, chip, core):
        pairs = [(i, 2 * ((i // 2 + chip) % chips) + ((i % 2) ^ core)) for i in range(tensor)]
        return lax.ppermute(x, "tensor", pairs)

    def cross(x):
        return {d: move(x, d, 0) for d in range(1, chips)}

    def spread(x, crossed):
        found = {(0, 0): x, (0, 1): move(x, 0, 1)}
        for d in range(1, chips):
            found[d, 0] = crossed[d]
        for d in range(1, chips):
            found[d, 1] = move(crossed[d], 0, 1)
        return found

    own = (
        jnp.einsum("rthn,hnc->rthc", q_nope, w_uk, preferred_element_type=f32)
        .astype(bf16)
        .reshape(requests, rows, width)
    )
    rope_rows = q_rope.reshape(requests, rows, rope_width)
    scales = spread(scale_pool, cross(scale_pool))
    ropes = spread(rope_rows, cross(rope_rows))
    halves = [own[h * half : (h + 1) * half] for h in range(requests // half)]
    crossed = [cross(x) for x in halves]
    query = [{(d, 0): crossed[h][d] for d in range(1, chips)} for h in range(len(halves))]
    for h in range(len(halves)):
        for d in range(1, chips):
            query[h][d, 1] = move(crossed[h][d], 0, 1)
    partner = move(own, 0, 1)
    table = jnp.stack(list(scales.values()))
    cache = prepare(0, requests, block_index, table, cache_latent, cache_rope)
    after = lengths
    backs = []
    for d in range(1, chips):
        for h in range(len(halves)):
            oa, ob, la, lb = attend(
                h * half, lengths, query[h][d, 0], query[h][d, 1], ropes[d, 0], ropes[d, 1], *cache, after, tokens, factor
            )
            after = la
            ob, lb = move(ob, 0, 1), move(lb, 0, 1)
            both = weigh(oa, ob, la, lb)
            backs.append(move(both, -d, 0))
    oa, ob, la, lb = attend(
        0, lengths, own, partner, ropes[0, 0], ropes[0, 1], *cache, after, tokens, factor
    )
    attended = finish(half, oa, move(ob, 0, 1), la, move(lb, 0, 1), backs)
    attended = attended.reshape(requests, tokens, heads, width)
    projected = jnp.einsum("rthc,hcv->rthv", attended, w_uv, preferred_element_type=f32)
    return projected.astype(bf16)


def solution(mesh):
    placed = (
        P("dp", None, "tensor", None),
        P("dp", None, "tensor", None),
        P("tensor", None, None),
        P("tensor", None, None),
        P("dp", "tensor", None),
        P("dp", None, "tensor"),
        P(None, ("dp", "tensor")),
        P("dp", "tensor"),
        P("dp"),
    )

    def body(*args):
        return local(mesh.shape["tensor"], *args)

    return jax.shard_map(
        body,
        mesh=mesh,
        in_specs=placed,
        out_specs=P("dp", None, "tensor", None),
        check_vma=False,
    )
```
